32 devices in a mesh: row: 8 (over y, x, core), col: 4 (over z).
Axes of the slice: x: 2, y: 2, z: 4, core: 2. Of those that a mesh axis runs over, the one named last changes fastest.
Arguments:
- tokens: bfloat16 [256, 2880], P('row', 'col'), may hold values from -6 to 6
- route_ids: int32 [256, 4], P('row'), may hold values from 0 to 15, all different within a row; in each aligned block of 32 rows (0 to 31, 32 to 63, ...) at most 8 rows name the same one
- route_weights: float32 [256, 4], P('row'), may hold values from 0.1 to 1
- expert_gate_up: bfloat16 [16, 2880, 2, 2880], P('row', None, None, 'col'), may hold values from -0.109375 to 0.109375
- expert_down: bfloat16 [16, 2880, 2880], P('row', 'col'), may hold values from -0.15625 to 0.15625
Outputs:
- moe_out: bfloat16 [256, 2880], P('row', 'col')
The draws below stay inside these ranges and needn't reach their ends.
Inputs may be any that keep to these rules, and one draw needn't show every extreme that they name: `route_ids`: each token names 4 different experts. Among the 32 tokens of one index of row, no expert is named more than 8 times, a bound that some block reaches.
All inputs are finite; a program needn't handle non-finite values.
Results may differ from the reference program's by a relative error of at most 0.0049.
Values may be sent and summed in bfloat16 or wider, within the bound.
No kernel may reach another device: no remote copies, remote signals or barrier semaphores. Data moves between devices by JAX's collectives and lax.ppermute only.
A program may use at most 256 MiB of HBM per device.

```python
import math
import jax
import jax.numpy as jnp
import numpy as np
from jax import lax

D = 2880
FF = 2880
TOP = 4
CAP = 8
TOK_ROW = 32
EXPERTS = 16
TOKENS = 256
N_ROW = 8


def strengthened(values, key, source, target, shards_of, factor):
    owner, partner = [(jnp.arange(values.shape[position]) // (values.shape[position] // shards_of)).reshape([-1 if axis == position else 1 for axis in range(values.ndim)]) for position in (source, target)]
    chosen = jax.random.permutation(key, shards_of)[partner]
    strong = (owner == chosen) | (owner == (partner + shards_of // 2) % shards_of)
    return jnp.where(strong, factor * values, values)


def levels(own_key, extent, split, smallest, largest):
    def one(axis_at, parts):
        draws = jax.random.uniform(jax.random.fold_in(jax.random.fold_in(own_key, 6), axis_at), (parts,), jnp.float32, smallest / len(split), largest / len(split))
        return jnp.repeat(jnp.exp(draws), extent[axis_at] // parts).reshape((-1,) + (1,) * (len(extent) - axis_at - 1))

    factor_of = one(*split[0])
    for cut in split[1:]:
        factor_of = factor_of * one(*cut)
    return factor_of


def shared_out(own_key, own, number, rows, count, top, most, slope):
    ranking = jax.random.permutation(own_key, count)
    packed, usual = portions_of(count, rows * top, most, slope, True), portions_of(count, rows * top, most, slope, False)
    places = jnp.arange(count)

    def named(sizes, offset_by):
        used = int((sizes > 0).sum())
        fixed = max(1, used // 4)
        passed = fixed + (places - fixed + offset_by * (used - fixed)) % max(1, count - fixed)
        return jnp.zeros((count,), jnp.int32).at[ranking[jnp.where(places < fixed, places, passed)]].set(jnp.asarray(sizes, jnp.int32))

    sizes = jnp.where(number % 4 == 0, named(packed, number // 4), named(usual, number - number // 4 - 1))
    mixed = jax.random.permutation(jax.random.fold_in(own, 3), count)
    giver, sink = mixed[0:count // 2 * 2:2], mixed[1:count // 2 * 2:2]
    room = jnp.minimum(sizes[giver] - 1, most - sizes[sink]) // 2
    room = jnp.where((giver == ranking[0]) | (sink == ranking[0]) | (sizes[sink] == 0), 0, jnp.maximum(room, 0))
    passed = jax.random.randint(jax.random.fold_in(own, 4), (count // 2,), 0, 1 << 20) % (room + 1)
    sizes = sizes.at[giver].add(-passed).at[sink].add(passed)
    members = jnp.searchsorted(jnp.cumsum(sizes), jnp.arange(rows * top), side="right").astype(jnp.int32)
    table = members.reshape(top, rows).T
    table = table[jax.random.permutation(jax.random.fold_in(own, 1), rows)]
    offset_by = jax.random.randint(jax.random.fold_in(own, 2), (rows, 1), 0, top)
    return jnp.take_along_axis(table, (jnp.arange(top)[None, :] + offset_by) % top, axis=1)


def portions_of(count, total, limit, lean, full):
    portions = [(1 << 20) // math.isqrt(rank ** lean) + 1 for rank in range(1, count + 1)]
    largest = limit if full else min(limit, max(-(-total // count), total * portions[0] // sum(portions)))
    least = 1 if total - largest >= count - 1 else 0
    given, spare = [largest] + [least] * (count - 1), total - largest - least * (count - 1)
    while spare > 0:
        free = [i for i in range(1, count) if given[i] < largest] or [i for i in range(1, count) if given[i] < limit]
        mass, remaining = sum([portions[i] for i in free]), spare
        for i in free:
            addition = min(limit - given[i], max(1, remaining * portions[i] // mass), spare)
            given[i] = given[i] + addition
            spare = spare - addition
    return np.array(given)


def gaussian(key, dims, scale, reach, split=(), held_as=jnp.bfloat16):
    drawn = scale * jax.random.normal(key, dims, jnp.float32)
    if split:
        drawn = drawn * levels(key, dims, split, -0.22, 0.18)
    return jnp.clip(drawn, -reach, reach).astype(held_as)


def noise_with(own_key, shape, scale, bound, pieces, heavy, kind=jnp.bfloat16):
    entries = scale * jax.random.normal(own_key, shape, jnp.float32)
    if pieces:
        entries = entries * levels(own_key, shape, pieces, -0.22, 0.18)
    return jnp.clip(strengthened(entries, jax.random.fold_in(own_key, 3), *heavy), -bound, bound).astype(kind)


def setup_inputs(seed: int = 0) -> dict:
    key_list = jax.random.split(jax.random.key(seed), 6)
    tokens = gaussian(key_list[0], (TOKENS, D), 1.0, 6.0, ((0, 8), (1, 4)))
    route_ids_keys = jax.random.split(jax.random.fold_in(key_list[1], 1), TOKENS // TOK_ROW)
    route_ids_turns = jax.random.permutation(jax.random.fold_in(key_list[1], 3), TOKENS // TOK_ROW)
    route_ids = jax.vmap(lambda own, number: shared_out(jax.random.fold_in(key_list[1], 2), own, number, TOK_ROW, EXPERTS, TOP, CAP, 2))(route_ids_keys, route_ids_turns).reshape((TOKENS, TOP))
    route_weights = jnp.clip(jnp.exp(math.log(1.0) - 2.3025851 * jax.random.uniform(key_list[2], (TOKENS, TOP), jnp.float32) ** levels(key_list[2], (TOKENS, TOP), ((0, 8),), -0.2, 0.2)), 0.1, 1.0)
    expert_gate_up = gaussian(key_list[3], (EXPERTS, D, 2, FF), D ** -0.5, 0.109375, ((0, 8), (3, 4)))
    expert_down = noise_with(key_list[4], (EXPERTS, FF, D), FF ** -0.5, 0.15625, ((0, 8), (1, 4)), (1, 2, 4, 2.0))
    return {"tokens": tokens, "route_ids": route_ids, "route_weights": route_weights, "expert_gate_up": expert_gate_up, "expert_down": expert_down}


def slots_of(route_ids):
    ids = route_ids.reshape(N_ROW, TOK_ROW * TOP)
    onehot = (ids[:, :, None] == jnp.arange(EXPERTS, dtype=jnp.int32)[None, None, :]).astype(jnp.int32)
    before = jnp.cumsum(onehot, axis=1) - onehot
    return jnp.sum(before * onehot, axis=2).reshape(-1).astype(jnp.int32)


def reference(tokens, route_ids, route_weights, expert_gate_up, expert_down):
    chosen = route_ids.reshape(-1).astype(jnp.int32)
    slot = slots_of(route_ids)
    pairs = jnp.arange(TOKENS * TOP, dtype=jnp.int32)
    token_index = (pairs // TOP).astype(jnp.int32)
    block = (pairs // (TOK_ROW * TOP)).astype(jnp.int32)
    target = (block * CAP + slot).astype(jnp.int32)
    buffer = jnp.zeros((EXPERTS, N_ROW * CAP, D), tokens.dtype)
    buffer = buffer.at[chosen, target].set(tokens[token_index])

    def one_expert(operands):
        rows, gate_up, down = operands
        act = jnp.dot(rows, gate_up.reshape(D, 2 * FF), preferred_element_type=jnp.float32)
        act = act.reshape(rows.shape[0], 2, FF)
        gate = act[:, 0, :]
        up = act[:, 1, :]
        hidden = ((up + 1.0) * gate * jax.nn.sigmoid(1.702 * gate)).astype(jnp.bfloat16)
        return jnp.dot(hidden, down, preferred_element_type=jnp.float32)

    expert_out = lax.map(one_expert, (buffer, expert_gate_up, expert_down))
    picked = expert_out[chosen, target].astype(jnp.float32)
    weighted = picked * route_weights.reshape(-1)[:, None].astype(jnp.float32)
    return jnp.sum(weighted.reshape(TOKENS, TOP, D), axis=1).astype(jnp.bfloat16)
```

```python
import functools

import jax
import jax.numpy as jnp
from jax import lax
from jax.experimental import pallas as pl
from jax.experimental.pallas import tpu as pltpu
from jax.sharding import PartitionSpec as P

CAP = 8
NT = (((1,), (1,)), ((), ()))
TN = (((0,), (0,)), ((), ()))
VMEM = pl.BlockSpec(memory_space=pltpu.VMEM)
HBM = pl.BlockSpec(memory_space=pltpu.HBM)


def dest(i, j, n):
    return i ^ j if n & (n - 1) == 0 else (i + j) % n


def source(i, j, n):
    return i ^ j if n & (n - 1) == 0 else (i + n - j) % n


def chunks_of(total, size):
    return [(at, min(size, total - at)) for at in range(0, total, size)]


def route_kernel(rows, exp_dev, ids_ref, w_ref, place_ref, high_ref, low_ref):
    pair = 2 if rows % 2 == 0 else 1
    chips = rows // pair
    me = lax.axis_index("row")
    top, toks = ids_ref.shape
    experts = rows * exp_dev
    at = lax.broadcasted_iota(jnp.int32, (experts, 1), 0)
    e, q, j = at // rows, (at // chips) % pair, at % chips
    chip = dest(jnp.full_like(at, me // pair), j, chips)
    core = jnp.full_like(at, me % pair) ^ q
    expert = (chip * pair + core) * exp_dev + e
    hit = jnp.zeros((experts, toks), jnp.float32)
    weight = jnp.zeros((experts, toks), jnp.float32)
    for k in range(top):
        same = (ids_ref[k : k + 1, :] == expert).astype(jnp.float32)
        hit += same
        weight += same * w_ref[k : k + 1, :]
    earlier = lax.broadcasted_iota(jnp.int32, (toks, toks), 0)
    later = lax.broadcasted_iota(jnp.int32, (toks, toks), 1)
    before = jnp.dot(
        hit.astype(jnp.bfloat16),
        (earlier < later).astype(jnp.bfloat16),
        preferred_element_type=jnp.float32,
    )
    slot = jnp.where(hit > 0.0, before, -1.0)
    spread = lambda a: jnp.broadcast_to(a[:, None, :], (experts, CAP, toks)).reshape(
        experts * CAP, toks
    )
    want = lax.broadcasted_iota(jnp.int32, (experts * CAP, toks), 0) % CAP
    place = (spread(slot) == want.astype(jnp.float32)).astype(jnp.float32)
    value = place * spread(weight)
    high = value.astype(jnp.bfloat16)
    place_ref[...] = place.astype(jnp.bfloat16)
    high_ref[...] = high
    low_ref[...] = (value - high.astype(jnp.float32)).astype(jnp.bfloat16)


def dispatch_kernel(cols, outs, place_ref, *refs):
    part_refs, out_refs, whole = refs[:cols], refs[cols : cols + outs], refs[-1]
    col = lax.axis_index("col")
    width = part_refs[0].shape[1]
    parts = [r[...] for r in part_refs]
    for p in range(cols):
        j = source(col, p, cols) if cols & (cols - 1) == 0 else (col + cols - p) % cols
        part = parts[0]
        for other in range(1, cols):
            part = jnp.where(j == other, parts[other], part)
        whole[:, p * width : (p + 1) * width] = part.astype(jnp.float32)
    full = whole[...].astype(jnp.bfloat16)
    sent = jnp.dot(place_ref[...], full, preferred_element_type=jnp.float32)
    sent = sent.astype(jnp.bfloat16)
    each = sent.shape[0] // outs
    for i in range(outs):
        out_refs[i][...] = sent[i * each : (i + 1) * each]


def expert_kernel(e, blocks, gu_hbm, dn_hbm, *refs):
    x_refs, y_refs = refs[:blocks], refs[blocks : 2 * blocks]
    gu, dn, x, hidden, sems = refs[2 * blocks :]
    hid, width = dn.shape
    steps = chunks_of(hid, 256)
    copies = []
    for i, (at, size) in enumerate(steps):
        for g in range(2):
            copies.append(
                pltpu.make_async_copy(
                    gu_hbm.at[e, g, pl.ds(at, size)],
                    gu.at[g, pl.ds(at, size)],
                    sems.at[2 * i + g],
                )
            )
    last = pltpu.make_async_copy(dn_hbm.at[e], dn, sems.at[2 * len(steps)])
    for c in copies:
        c.start()
    last.start()
    rows = x_refs[0].shape[0]
    for b in range(blocks):
        x[b * rows : (b + 1) * rows] = x_refs[b][...]
    for i, (at, size) in enumerate(steps):
        copies[2 * i].wait()
        gate = lax.dot_general(
            x[...], gu[0, at : at + size], NT, preferred_element_type=jnp.float32
        )
        copies[2 * i + 1].wait()
        up = lax.dot_general(
            x[...], gu[1, at : at + size], NT, preferred_element_type=jnp.float32
        )
        act = (up + 1.0) * gate * jax.nn.sigmoid(1.702 * gate)
        hidden[:, at : at + size] = act.astype(jnp.bfloat16)
    last.wait()
    for at, size in chunks_of(width, 768):
        part = jnp.dot(
            hidden[...], dn[:, at : at + size], preferred_element_type=jnp.float32
        ).astype(jnp.bfloat16)
        for b in range(blocks):
            y_refs[b][:, at : at + size] = part[b * rows : (b + 1) * rows]


def combine_kernel(exp_dev, chips, pair, cols, high_ref, low_ref, *refs):
    per = chips + (pair - 1)
    ins, refs = refs[: exp_dev * per], refs[exp_dev * per :]
    own_ref, out_refs, flat, mixed = refs[0], refs[1:cols], refs[-2], refs[-1]
    col = lax.axis_index("col")
    at = 0
    for e in range(exp_dev):
        for j in range(chips):
            flat[at : at + CAP] = ins[e * per + j][:CAP]
            at += CAP
        if pair == 2:
            flat[at : at + CAP * chips] = ins[e * per + chips][...]
            at += CAP * chips
    y = flat[...]
    total = lax.dot_general(high_ref[...], y, TN, preferred_element_type=jnp.float32)
    total += lax.dot_general(low_ref[...], y, TN, preferred_element_type=jnp.float32)
    width = own_ref.shape[1]
    for p in range(cols):
        mixed[p] = total[:, p * width : (p + 1) * width]
    own_ref[...] = mixed[col]
    for j in range(1, cols):
        out_refs[j - 1][...] = mixed[dest(col, j, cols)].astype(jnp.bfloat16)


def params(mib):
    return pltpu.CompilerParams(vmem_limit_bytes=mib << 20)


def on_device(tokens, route_ids, route_weights, expert_gate_up, expert_down):
    rows, cols = lax.axis_size("row"), lax.axis_size("col")
    pair = 2 if rows % 2 == 0 else 1
    chips = rows // pair
    toks, part_width = tokens.shape
    exp_dev, width, _, hid = expert_gate_up.shape
    slots = exp_dev * rows * CAP
    bf16, f32 = jnp.bfloat16, jnp.float32
    shape = jax.ShapeDtypeStruct

    def over_col(x, j):
        return lax.ppermute(x, "col", [(i, dest(i, j, cols)) for i in range(cols)])

    def over_chips(x, j, back=False):
        to = source if back else dest
        perm = [
            (c * pair + k, to(c, j, chips) * pair + k)
            for c in range(chips)
            for k in range(pair)
        ]
        return lax.ppermute(x, "row", perm)

    def over_cores(x):
        return lax.ppermute(x, "row", [(i, i ^ 1) for i in range(rows)])

    far = list(range(cols - 1, 0, -1))
    arrived = {j: over_col(tokens, j) for j in far}
    parts = [tokens] + [arrived[j] for j in range(1, cols)]

    place, high, low = pl.pallas_call(
        functools.partial(route_kernel, rows, exp_dev),
        out_shape=[shape((slots, toks), bf16)] * 3,
        in_specs=[VMEM] * 2,
        out_specs=[VMEM] * 3,
        compiler_params=params(4),
        name="route",
    )(route_ids.T, route_weights.T)

    outs = exp_dev * pair
    sent = pl.pallas_call(
        functools.partial(dispatch_kernel, cols, outs),
        out_shape=[shape((chips * CAP, width), bf16)] * outs,
        in_specs=[VMEM] * (1 + cols),
        out_specs=[VMEM] * outs,
        scratch_shapes=[pltpu.VMEM((toks, width), f32)],
        compiler_params=params(8),
        name="dispatch",
    )(place, *parts)

    gate_up = jnp.transpose(expert_gate_up, (0, 2, 3, 1))
    block = pair * CAP
    n_copies = 2 * len(chunks_of(hid, 256)) + 1
    inputs = []
    for e in range(exp_dev):
        halves = [sent[e * pair].reshape(chips, CAP, width)]
        if pair == 2:
            halves.append(over_cores(sent[e * pair + 1]).reshape(chips, CAP, width))
        blocks = [
            jnp.concatenate([h[j] for h in halves], axis=0) for j in range(chips)
        ]
        inputs.append(
            {0: blocks[0]}
            | {j: over_chips(blocks[j], j) for j in range(chips - 1, 0, -1)}
        )
    terms = []
    for e in range(exp_dev):
        ys = pl.pallas_call(
            functools.partial(expert_kernel, e, chips),
            out_shape=[shape((block, width), bf16)] * chips,
            in_specs=[HBM] * 2 + [VMEM] * chips,
            out_specs=[VMEM] * chips,
            scratch_shapes=[
                pltpu.VMEM((2, hid, width), bf16),
                pltpu.VMEM((hid, width), bf16),
                pltpu.VMEM((chips * block, width), bf16),
                pltpu.VMEM((chips * block, hid), bf16),
                pltpu.SemaphoreType.DMA((n_copies,)),
            ],
            compiler_params=params(24),
            cost_estimate=pl.CostEstimate(
                flops=6 * chips * block * width * hid,
                bytes_accessed=6 * width * hid,
                transcendentals=chips * block * hid,
            ),
            name=f"expert{e}",
        )(gate_up, expert_down, *[inputs[e][j] for j in range(chips)])
        back = {0: ys[0]} | {
            j: over_chips(ys[j], j, True) for j in range(chips - 1, 0, -1)
        }
        got = [back[j] for j in range(chips)]
        terms += got
        if pair == 2:
            give = jnp.concatenate([g[CAP:] for g in got], axis=0)
            terms.append(over_cores(give))

    own, *leaving = pl.pallas_call(
        functools.partial(combine_kernel, exp_dev, chips, pair, cols),
        out_shape=[shape((toks, part_width), f32)]
        + [shape((toks, part_width), bf16)] * (cols - 1),
        in_specs=[VMEM] * (2 + len(terms)),
        out_specs=[VMEM] * cols,
        scratch_shapes=[
            pltpu.VMEM((slots, width), bf16),
            pltpu.VMEM((cols, toks, part_width), f32),
        ],
        compiler_params=params(16),
        name="combine",
    )(high, low, *terms)
    total = own
    for j in far:
        total = total + over_col(leaving[j - 1], j).astype(f32)
    return total.astype(bf16)


def solution(mesh):
    return jax.shard_map(
        on_device,
        mesh=mesh,
        in_specs=(
            P("row", "col"),
            P("row", None),
            P("row", None),
            P("row", None, None, "col"),
            P("row", "col", None),
        ),
        out_specs=P("row", "col"),
        check_vma=False,
    )
```

```python
import functools

import jax
import jax.numpy as jnp
from jax import lax
from jax.experimental import pallas as pl
from jax.experimental.pallas import tpu as pltpu
from jax.sharding import PartitionSpec as P

CAP = 8
NT = (((1,), (1,)), ((), ()))
TN = (((0,), (0,)), ((), ()))
VMEM = pl.BlockSpec(memory_space=pltpu.VMEM)
HBM = pl.BlockSpec(memory_space=pltpu.HBM)


def dest(i, j, n):
    return i ^ j if n & (n - 1) == 0 else (i + j) % n


def source(i, j, n):
    return i ^ j if n & (n - 1) == 0 else (i + n - j) % n


def chunks_of(total, size):
    return [(at, min(size, total - at)) for at in range(0, total, size)]


def fetches(e, gu_hbm, dn_hbm, gu, dn, sems):
    return [
        pltpu.make_async_copy(gu_hbm.at[e], gu, sems.at[0]),
        pltpu.make_async_copy(dn_hbm.at[e], dn, sems.at[1]),
    ]


def route_kernel(rows, exp_dev, ids_ref, w_ref, gu_hbm, dn_hbm, *refs):
    place_ref, high_ref, low_ref, gu, dn, *_, sems = refs
    copies = fetches(0, gu_hbm, dn_hbm, gu, dn, sems)
    for c in copies:
        c.start()
    pair = 2 if rows % 2 == 0 else 1
    chips = rows // pair
    me = lax.axis_index("row")
    top, toks = ids_ref.shape
    experts = rows * exp_dev
    at = lax.broadcasted_iota(jnp.int32, (experts, 1), 0)
    e, q, j = at // rows, (at // chips) % pair, at % chips
    chip = dest(jnp.full_like(at, me // pair), j, chips)
    core = jnp.full_like(at, me % pair) ^ q
    expert = (chip * pair + core) * exp_dev + e
    hit = jnp.zeros((experts, toks), jnp.float32)
    weight = jnp.zeros((experts, toks), jnp.float32)
    for k in range(top):
        same = (ids_ref[k : k + 1, :] == expert).astype(jnp.float32)
        hit += same
        weight += same * w_ref[k : k + 1, :]
    earlier = lax.broadcasted_iota(jnp.int32, (toks, toks), 0)
    later = lax.broadcasted_iota(jnp.int32, (toks, toks), 1)
    before = jnp.dot(
        hit.astype(jnp.bfloat16),
        (earlier < later).astype(jnp.bfloat16),
        preferred_element_type=jnp.float32,
    )
    slot = jnp.where(hit > 0.0, before, -1.0)
    spread = lambda a: jnp.broadcast_to(a[:, None, :], (experts, CAP, toks)).reshape(
        experts * CAP, toks
    )
    want = lax.broadcasted_iota(jnp.int32, (experts * CAP, toks), 0) % CAP
    place = (spread(slot) == want.astype(jnp.float32)).astype(jnp.float32)
    value = place * spread(weight)
    high = value.astype(jnp.bfloat16)
    place_ref[...] = place.astype(jnp.bfloat16)
    high_ref[...] = high
    low_ref[...] = (value - high.astype(jnp.float32)).astype(jnp.bfloat16)
    for c in copies:
        c.wait()


def dispatch_kernel(cols, outs, place_ref, *refs):
    part_refs, out_refs, whole = refs[:cols], refs[cols : cols + outs], refs[-1]
    col = lax.axis_index("col")
    width = part_refs[0].shape[1]
    parts = [r[...] for r in part_refs]
    for p in range(cols):
        j = source(col, p, cols) if cols & (cols - 1) == 0 else (col + cols - p) % cols
        part = parts[0]
        for other in range(1, cols):
            part = jnp.where(j == other, parts[other], part)
        whole[:, p * width : (p + 1) * width] = part.astype(jnp.float32)
    full = whole[...].astype(jnp.bfloat16)
    sent = jnp.dot(place_ref[...], full, preferred_element_type=jnp.float32)
    sent = sent.astype(jnp.bfloat16)
    each = sent.shape[0] // outs
    for i in range(outs):
        out_refs[i][...] = sent[i * each : (i + 1) * each]


def expert_kernel(e, blocks, more, *refs):
    gu, dn = refs[:2]
    refs = refs[2:]
    copies = []
    if more:
        copies = fetches(e + 1, *refs[:2], *refs[-5:-3], refs[-1])
        refs = refs[4:-1]
    for c in copies:
        c.start()
    x_refs, y_refs = refs[:blocks], refs[blocks : 2 * blocks]
    x, hidden = refs[-2:]
    hid, width = dn.shape
    rows = x_refs[0].shape[0]
    for b in range(blocks):
        x[b * rows : (b + 1) * rows] = x_refs[b][...]
    for at, size in chunks_of(hid, 256):
        gate, up = [
            lax.dot_general(
                x[...], gu[g, at : at + size], NT, preferred_element_type=jnp.float32
            )
            for g in range(2)
        ]
        act = (up + 1.0) * gate * jax.nn.sigmoid(1.702 * gate)
        hidden[:, at : at + size] = act.astype(jnp.bfloat16)
    for at, size in chunks_of(width, 768):
        part = jnp.dot(
            hidden[...], dn[:, at : at + size], preferred_element_type=jnp.float32
        ).astype(jnp.bfloat16)
        for b in range(blocks):
            y_refs[b][:, at : at + size] = part[b * rows : (b + 1) * rows]
    for c in copies:
        c.wait()


def combine_kernel(exp_dev, chips, pair, cols, high_ref, low_ref, *refs):
    per = chips + (pair - 1)
    ins, refs = refs[: exp_dev * per], refs[exp_dev * per :]
    own_ref, out_refs, flat, mixed = refs[0], refs[1:cols], refs[-2], refs[-1]
    col = lax.axis_index("col")
    at = 0
    for e in range(exp_dev):
        for j in range(chips):
            flat[at : at + CAP] = ins[e * per + j][:CAP]
            at += CAP
        if pair == 2:
            flat[at : at + CAP * chips] = ins[e * per + chips][...]
            at += CAP * chips
    y = flat[...]
    total = lax.dot_general(high_ref[...], y, TN, preferred_element_type=jnp.float32)
    total += lax.dot_general(low_ref[...], y, TN, preferred_element_type=jnp.float32)
    width = own_ref.shape[1]
    for p in range(cols):
        mixed[p] = total[:, p * width : (p + 1) * width]
    own_ref[...] = mixed[col]
    for j in range(1, cols):
        out_refs[j - 1][...] = mixed[dest(col, j, cols)].astype(jnp.bfloat16)


def room(held_bytes):
    return pltpu.CompilerParams(vmem_limit_bytes=(58 << 20) - held_bytes)


def params(mib):
    return pltpu.CompilerParams(vmem_limit_bytes=mib << 20)


def on_device(tokens, route_ids, route_weights, expert_gate_up, expert_down):
    rows, cols = lax.axis_size("row"), lax.axis_size("col")
    pair = 2 if rows % 2 == 0 else 1
    chips = rows // pair
    toks, part_width = tokens.shape
    exp_dev, width, _, hid = expert_gate_up.shape
    slots = exp_dev * rows * CAP
    bf16, f32 = jnp.bfloat16, jnp.float32
    shape = jax.ShapeDtypeStruct

    def over_col(x, j):
        return lax.ppermute(x, "col", [(i, dest(i, j, cols)) for i in range(cols)])

    def over_chips(x, j, back=False):
        to = source if back else dest
        perm = [
            (c * pair + k, to(c, j, chips) * pair + k)
            for c in range(chips)
            for k in range(pair)
        ]
        return lax.ppermute(x, "row", perm)

    def over_cores(x):
        return lax.ppermute(x, "row", [(i, i ^ 1) for i in range(rows)])

    far = list(range(cols - 1, 0, -1))
    arrived = {j: over_col(tokens, j) for j in far}
    parts = [tokens] + [arrived[j] for j in range(1, cols)]

    gate_up = pltpu.with_memory_space_constraint(
        jnp.transpose(expert_gate_up, (0, 2, 3, 1)), pltpu.HBM
    )
    expert_down = pltpu.with_memory_space_constraint(expert_down, pltpu.HBM)
    held = [pltpu.VMEM((2, hid, width), bf16), pltpu.VMEM((hid, width), bf16)]
    held_bytes = 6 * hid * width
    place, high, low, *weights = pl.pallas_call(
        functools.partial(route_kernel, rows, exp_dev),
        out_shape=[shape((slots, toks), bf16)] * 3 + held * exp_dev,
        in_specs=[VMEM] * 2 + [HBM] * 2,
        out_specs=[VMEM] * (3 + 2 * exp_dev),
        scratch_shapes=[pltpu.SemaphoreType.DMA((2,))],
        compiler_params=params(16),
        name="route",
    )(route_ids.T, route_weights.T, gate_up, expert_down)

    outs = exp_dev * pair
    sent = pl.pallas_call(
        functools.partial(dispatch_kernel, cols, outs),
        out_shape=[shape((chips * CAP, width), bf16)] * outs,
        in_specs=[VMEM] * (1 + cols),
        out_specs=[VMEM] * outs,
        scratch_shapes=[pltpu.VMEM((toks, width), f32)],
        compiler_params=params(8),
        name="dispatch",
    )(place, *parts)

    block = pair * CAP
    inputs = []
    for e in range(exp_dev):
        halves = [sent[e * pair].reshape(chips, CAP, width)]
        if pair == 2:
            halves.append(over_cores(sent[e * pair + 1]).reshape(chips, CAP, width))
        blocks = [
            jnp.concatenate([h[j] for h in halves], axis=0) for j in range(chips)
        ]
        inputs.append(
            {0: blocks[0]}
            | {j: over_chips(blocks[j], j) for j in range(chips - 1, 0, -1)}
        )
    terms = []
    for e in range(exp_dev):
        more = e + 1 < exp_dev
        ys = pl.pallas_call(
            functools.partial(expert_kernel, e, chips, more),
            out_shape=[shape((block, width), bf16)] * chips + held * more,
            in_specs=[VMEM] * 2 + [HBM, HBM, VMEM, VMEM] * more + [VMEM] * chips,
            out_specs=[VMEM] * (chips + 2 * more),
            scratch_shapes=[
                pltpu.VMEM((chips * block, width), bf16),
                pltpu.VMEM((chips * block, hid), bf16),
            ]
            + [pltpu.SemaphoreType.DMA((2,))] * more,
            compiler_params=params(16),
            cost_estimate=pl.CostEstimate(
                flops=6 * chips * block * width * hid,
                bytes_accessed=6 * width * hid,
                transcendentals=chips * block * hid,
            ),
            input_output_aliases={4: chips, 5: chips + 1} if more else {},
            name=f"expert{e}",
        )(
            *weights[:2],
            *[gate_up, expert_down, *weights[2:4]] * more,
            *[inputs[e][j] for j in range(chips)],
        )
        weights = [*ys[chips:], *weights[4:]]
        back = {0: ys[0]} | {
            j: over_chips(ys[j], j, True) for j in range(chips - 1, 0, -1)
        }
        got = [back[j] for j in range(chips)]
        terms += got
        if pair == 2:
            give = jnp.concatenate([g[CAP:] for g in got], axis=0)
            terms.append(over_cores(give))

    own, *leaving = pl.pallas_call(
        functools.partial(combine_kernel, exp_dev, chips, pair, cols),
        out_shape=[shape((toks, part_width), f32)]
        + [shape((toks, part_width), bf16)] * (cols - 1),
        in_specs=[VMEM] * (2 + len(terms)),
        out_specs=[VMEM] * cols,
        scratch_shapes=[
            pltpu.VMEM((slots, width), bf16),
            pltpu.VMEM((cols, toks, part_width), f32),
        ],
        compiler_params=params(16),
        name="combine",
    )(high, low, *terms)
    total = own
    for j in far:
        total = total + over_col(leaving[j - 1], j).astype(f32)
    return total.astype(bf16)


def solution(mesh):
    return jax.shard_map(
        on_device,
        mesh=mesh,
        in_specs=(
            P("row", "col"),
            P("row", None),
            P("row", None),
            P("row", None, None, "col"),
            P("row", "col", None),
        ),
        out_specs=P("row", "col"),
        check_vma=False,
    )
```

```python
import functools

import jax
import jax.numpy as jnp
from jax import lax
from jax.experimental import pallas as pl
from jax.experimental.pallas import tpu as pltpu
from jax.sharding import PartitionSpec as P


CAP = 8
NT = (((1,), (1,)), ((), ()))
TN = (((0,), (0,)), ((), ()))
VMEM = pl.BlockSpec(memory_space=pltpu.VMEM)
HBM = pl.BlockSpec(memory_space=pltpu.HBM)


def dest(i, j, n):
    return i ^ j if n & (n - 1) == 0 else (i + j) % n


def source(i, j, n):
    return i ^ j if n & (n - 1) == 0 else (i + n - j) % n


def chunks_of(total, size):
    return [(at, min(size, total - at)) for at in range(0, total, size)]


def fetches(e, gu_hbm, dn_hbm, gu, dn, sems):
    return [
        pltpu.make_async_copy(gu_hbm.at[e], gu, sems.at[0]),
        pltpu.make_async_copy(dn_hbm.at[e], dn, sems.at[1]),
    ]


def route_kernel(rows, exp_dev, ids_hbm, w_hbm, gu_hbm, dn_hbm, *refs):
    place_ref, high_ref, low_ref, gu, dn, ids_ref, w_ref, sems = refs
    small = [
        pltpu.make_async_copy(ids_hbm, ids_ref, sems.at[2]),
        pltpu.make_async_copy(w_hbm, w_ref, sems.at[3]),
    ]
    copies = fetches(0, gu_hbm, dn_hbm, gu, dn, sems)
    for c in small + copies:
        c.start()
    pair = 2 if rows % 2 == 0 else 1
    chips = rows // pair
    me = lax.axis_index("row")
    top, toks = ids_ref.shape
    experts = rows * exp_dev
    at = lax.broadcasted_iota(jnp.int32, (experts, 1), 0)
    q, j, e = at // (chips * exp_dev), (at // exp_dev) % chips, at % exp_dev
    chip = dest(jnp.full_like(at, me // pair), j, chips)
    core = jnp.full_like(at, me % pair) ^ q
    expert = (chip * pair + core) * exp_dev + e
    hit = jnp.zeros((experts, toks), jnp.float32)
    weight = jnp.zeros((experts, toks), jnp.float32)
    for c in small:
        c.wait()
    for k in range(top):
        same = (ids_ref[k : k + 1, :] == expert).astype(jnp.float32)
        hit += same
        weight += same * w_ref[k : k + 1, :]
    earlier = lax.broadcasted_iota(jnp.int32, (toks, toks), 0)
    later = lax.broadcasted_iota(jnp.int32, (toks, toks), 1)
    before = jnp.dot(
        hit.astype(jnp.bfloat16),
        (earlier < later).astype(jnp.bfloat16),
        preferred_element_type=jnp.float32,
    )
    slot = jnp.where(hit > 0.0, before, -1.0)
    spread = lambda a: jnp.broadcast_to(a[:, None, :], (experts, CAP, toks)).reshape(
        experts * CAP, toks
    )
    want = lax.broadcasted_iota(jnp.int32, (experts * CAP, toks), 0) % CAP
    place = (spread(slot) == want.astype(jnp.float32)).astype(jnp.float32)
    value = place * spread(weight)
    high = value.astype(jnp.bfloat16)
    place_ref[...] = place.astype(jnp.bfloat16)
    high_ref[...] = high
    low_ref[...] = (value - high.astype(jnp.float32)).astype(jnp.bfloat16)
    for c in copies:
        c.wait()


def dispatch_kernel(cols, outs, place_ref, *refs):
    part_refs, out_refs, whole = refs[:cols], refs[cols : cols + outs], refs[-1]
    col = lax.axis_index("col")
    width = part_refs[0].shape[1]
    parts = [r[...] for r in part_refs]
    for p in range(cols):
        j = source(col, p, cols) if cols & (cols - 1) == 0 else (col + cols - p) % cols
        part = parts[0]
        for other in range(1, cols):
            part = jnp.where(j == other, parts[other], part)
        whole[:, p * width : (p + 1) * width] = part.astype(jnp.float32)
    full = whole[...].astype(jnp.bfloat16)
    sent = jnp.dot(place_ref[...], full, preferred_element_type=jnp.float32)
    sent = sent.astype(jnp.bfloat16)
    at = 0
    for out in out_refs:
        out[...] = sent[at : at + out.shape[0]]
        at += out.shape[0]


def experts_kernel(exp_dev, blocks, gu_hbm, dn_hbm, gu0, dn0, *refs):
    x_refs, y_refs = refs[:blocks], refs[blocks : 2 * blocks]
    x, hidden, *held, sems = refs[2 * blocks :]
    gus, dns = [gu0, *held[0::2]], [dn0, *held[1::2]]
    copies = [
        fetches(e, gu_hbm, dn_hbm, gus[e], dns[e], sems.at[pl.ds(2 * e, 2)])
        for e in range(1, exp_dev)
    ]
    for pair in copies:
        for c in pair:
            c.start()
    hid, width = dn0.shape
    for e in range(exp_dev):
        gu, dn, rows = gus[e], dns[e], slice(e * CAP, (e + 1) * CAP)
        for b in range(blocks):
            x[b * CAP : (b + 1) * CAP] = x_refs[b][rows]
        if e:
            copies[e - 1][0].wait()
        for at, size in chunks_of(hid, 256):
            gate, up = [
                lax.dot_general(
                    x[...],
                    gu[g, at : at + size],
                    NT,
                    preferred_element_type=jnp.float32,
                )
                for g in range(2)
            ]
            act = (up + 1.0) * gate * jax.nn.sigmoid(1.702 * gate)
            hidden[:, at : at + size] = act.astype(jnp.bfloat16)
        if e:
            copies[e - 1][1].wait()
        for at, size in chunks_of(width, 768):
            part = jnp.dot(
                hidden[...], dn[:, at : at + size], preferred_element_type=jnp.float32
            ).astype(jnp.bfloat16)
            for b in range(blocks):
                y_refs[b][rows, at : at + size] = part[b * CAP : (b + 1) * CAP]


def combine_kernel(cols, pieces, high_ref, low_ref, *refs):
    ins, refs = refs[:pieces], refs[pieces:]
    own_ref, out_refs, flat, mixed = refs[0], refs[1:cols], refs[-2], refs[-1]
    col = lax.axis_index("col")
    at = 0
    for piece in ins:
        flat[at : at + piece.shape[0]] = piece[...]
        at += piece.shape[0]
    y = flat[...]
    total = lax.dot_general(high_ref[...], y, TN, preferred_element_type=jnp.float32)
    total += lax.dot_general(low_ref[...], y, TN, preferred_element_type=jnp.float32)
    width = own_ref.shape[1]
    for p in range(cols):
        mixed[p] = total[:, p * width : (p + 1) * width]
    own_ref[...] = mixed[col]
    for j in range(1, cols):
        out_refs[j - 1][...] = mixed[dest(col, j, cols)].astype(jnp.bfloat16)


def params(mib):
    return pltpu.CompilerParams(vmem_limit_bytes=mib << 20)


def layer(tokens, route_ids, route_weights, expert_gate_up, expert_down):
    rows, cols = lax.axis_size("row"), lax.axis_size("col")
    pair = 2 if rows % 2 == 0 else 1
    chips = rows // pair
    toks, part_width = tokens.shape
    exp_dev, width, _, hid = expert_gate_up.shape
    slots = exp_dev * rows * CAP
    block = exp_dev * CAP
    bf16, f32 = jnp.bfloat16, jnp.float32
    shape = jax.ShapeDtypeStruct

    def over_col(x, j):
        return lax.ppermute(x, "col", [(i, dest(i, j, cols)) for i in range(cols)])

    def over_chips(x, j, back=False):
        to = source if back else dest
        perm = [
            (c * pair + k, to(c, j, chips) * pair + k)
            for c in range(chips)
            for k in range(pair)
        ]
        return lax.ppermute(x, "row", perm)

    def over_cores(x):
        return lax.ppermute(x, "row", [(i, i ^ 1) for i in range(rows)])

    def hold(x):
        return pltpu.with_memory_space_constraint(x, pltpu.HBM)

    far = range(cols - 1, 0, -1)
    arrived = {j: over_col(tokens, j) for j in far}
    parts = [tokens] + [arrived[j] for j in range(1, cols)]

    gate_up = hold(jnp.transpose(expert_gate_up, (0, 2, 3, 1)))
    expert_down = hold(expert_down)
    held = [((2, hid, width), bf16), ((hid, width), bf16)]
    place, high, low, gu, dn = pl.pallas_call(
        functools.partial(route_kernel, rows, exp_dev),
        out_shape=[shape((slots, toks), bf16)] * 3 + [pltpu.VMEM(*h) for h in held],
        in_specs=[HBM] * 4,
        out_specs=[VMEM] * 5,
        scratch_shapes=[
            pltpu.VMEM(route_ids.shape[::-1], route_ids.dtype),
            pltpu.VMEM(route_weights.shape[::-1], f32),
            pltpu.SemaphoreType.DMA((4,)),
        ],
        compiler_params=params(4),
        name="route",
    )(hold(route_ids.T), hold(route_weights.T), gate_up, expert_down)

    outs = chips + (pair - 1)
    dispatched = pl.pallas_call(
        functools.partial(dispatch_kernel, cols, outs),
        out_shape=[shape((block, width), bf16)] * chips
        + [shape((chips * block, width), bf16)] * (pair - 1),
        in_specs=[VMEM] * (1 + cols),
        out_specs=[VMEM] * outs,
        scratch_shapes=[pltpu.VMEM((toks, width), f32)],
        compiler_params=params(8),
        name="dispatch",
    )(place, *parts)

    keep, give = dispatched[:chips], dispatched[chips:]
    others = range(1, chips)
    inputs = [keep[0]] + [over_chips(keep[j], j) for j in others]
    if pair == 2:
        got = over_cores(give[0])
        got = [got[j * block : (j + 1) * block] for j in range(chips)]
        inputs += [got[0]] + [over_chips(got[j], j) for j in others]

    n = len(inputs)
    ys = pl.pallas_call(
        functools.partial(experts_kernel, exp_dev, n),
        out_shape=[shape((block, width), bf16)] * n,
        in_specs=[HBM] * 2 + [VMEM] * (2 + n),
        out_specs=[VMEM] * n,
        scratch_shapes=[
            pltpu.VMEM((n * CAP, width), bf16),
            pltpu.VMEM((n * CAP, hid), bf16),
        ]
        + [pltpu.VMEM(*h) for h in held] * (exp_dev - 1)
        + [pltpu.SemaphoreType.DMA((2 * exp_dev,))],
        compiler_params=params(24),
        cost_estimate=pl.CostEstimate(
            flops=6 * exp_dev * n * CAP * width * hid,
            bytes_accessed=6 * exp_dev * width * hid,
            transcendentals=exp_dev * n * CAP * hid,
        ),
        name="experts",
    )(gate_up, expert_down, gu, dn, *inputs)

    terms = []
    if pair == 2:
        back = [over_chips(ys[chips + j], j, True) for j in others]
        passed = jnp.concatenate([ys[chips], *back], axis=0)
        terms = [over_cores(passed)]
    near = [over_chips(ys[j], j, True) for j in others]
    terms = [ys[0], *near, *terms]

    own, *leaving = pl.pallas_call(
        functools.partial(combine_kernel, cols, len(terms)),
        out_shape=[shape((toks, part_width), f32)]
        + [shape((toks, part_width), bf16)] * (cols - 1),
        in_specs=[VMEM] * (2 + len(terms)),
        out_specs=[VMEM] * cols,
        scratch_shapes=[
            pltpu.VMEM((slots, width), bf16),
            pltpu.VMEM((cols, toks, part_width), f32),
        ],
        compiler_params=params(16),
        name="combine",
    )(high, low, *terms)
    total = own
    for j in far:
        total = total + over_col(leaving[j - 1], j).astype(f32)
    return total.astype(bf16)


def solution(mesh):
    return jax.shard_map(
        layer,
        mesh=mesh,
        in_specs=(
            P("row", "col"),
            P("row", None),
            P("row", None),
            P("row", None, None, "col"),
            P("row", "col", None),
        ),
        out_specs=P("row", "col"),
        check_vma=False,
    )
```

```python
import functools

import jax
import jax.numpy as jnp
from jax import lax
from jax.experimental import pallas as pl
from jax.experimental.pallas import tpu as pltpu
from jax.sharding import PartitionSpec as P


CAP = 8
NT = (((1,), (1,)), ((), ()))
TN = (((0,), (0,)), ((), ()))
VMEM = pl.BlockSpec(memory_space=pltpu.VMEM)
HBM = pl.BlockSpec(memory_space=pltpu.HBM)


def dest(i, j, n):
    return i ^ j if n & (n - 1) == 0 else (i + j) % n


def source(i, j, n):
    return i ^ j if n & (n - 1) == 0 else (i + n - j) % n


def chunks_of(total, size):
    return [(at, min(size, total - at)) for at in range(0, total, size)]


def fetches(e, gu_hbm, dn_hbm, gu, dn, sems):
    return [
        pltpu.make_async_copy(gu_hbm.at[e], gu, sems.at[0]),
        pltpu.make_async_copy(dn_hbm.at[e], dn, sems.at[1]),
    ]


def route_kernel(rows, exp_dev, ids_hbm, w_hbm, gu_hbm, dn_hbm, *refs):
    place_ref, high_ref, low_ref, gu, dn, *_, ids_ref, w_ref, sems = refs
    small = [
        pltpu.make_async_copy(ids_hbm, ids_ref, sems.at[2]),
        pltpu.make_async_copy(w_hbm, w_ref, sems.at[3]),
    ]
    copies = fetches(0, gu_hbm, dn_hbm, gu, dn, sems)
    for c in small + copies:
        c.start()
    pair = 2 if rows % 2 == 0 else 1
    chips = rows // pair
    me = lax.axis_index("row")
    top, toks = ids_ref.shape
    experts = rows * exp_dev
    at = lax.broadcasted_iota(jnp.int32, (experts, 1), 0)
    e, q, j = at // rows, (at // chips) % pair, at % chips
    chip = dest(jnp.full_like(at, me // pair), j, chips)
    core = jnp.full_like(at, me % pair) ^ q
    expert = (chip * pair + core) * exp_dev + e
    hit = jnp.zeros((experts, toks), jnp.float32)
    weight = jnp.zeros((experts, toks), jnp.float32)
    for c in small:
        c.wait()
    for k in range(top):
        same = (ids_ref[k : k + 1, :] == expert).astype(jnp.float32)
        hit += same
        weight += same * w_ref[k : k + 1, :]
    earlier = lax.broadcasted_iota(jnp.int32, (toks, toks), 0)
    later = lax.broadcasted_iota(jnp.int32, (toks, toks), 1)
    before = jnp.dot(
        hit.astype(jnp.bfloat16),
        (earlier < later).astype(jnp.bfloat16),
        preferred_element_type=jnp.float32,
    )
    slot = jnp.where(hit > 0.0, before, -1.0)
    spread = lambda a: jnp.broadcast_to(a[:, None, :], (experts, CAP, toks)).reshape(
        experts * CAP, toks
    )
    want = lax.broadcasted_iota(jnp.int32, (experts * CAP, toks), 0) % CAP
    place = (spread(slot) == want.astype(jnp.float32)).astype(jnp.float32)
    value = place * spread(weight)
    high = value.astype(jnp.bfloat16)
    place_ref[...] = place.astype(jnp.bfloat16)
    high_ref[...] = high
    low_ref[...] = (value - high.astype(jnp.float32)).astype(jnp.bfloat16)
    for c in copies:
        c.wait()


def dispatch_kernel(cols, outs, place_ref, *refs):
    part_refs, out_refs, whole = refs[:cols], refs[cols : cols + outs], refs[-1]
    col = lax.axis_index("col")
    width = part_refs[0].shape[1]
    parts = [r[...] for r in part_refs]
    for p in range(cols):
        j = source(col, p, cols) if cols & (cols - 1) == 0 else (col + cols - p) % cols
        part = parts[0]
        for other in range(1, cols):
            part = jnp.where(j == other, parts[other], part)
        whole[:, p * width : (p + 1) * width] = part.astype(jnp.float32)
    full = whole[...].astype(jnp.bfloat16)
    sent = jnp.dot(place_ref[...], full, preferred_element_type=jnp.float32)
    sent = sent.astype(jnp.bfloat16)
    each = sent.shape[0] // outs
    for i in range(outs):
        out_refs[i][...] = sent[i * each : (i + 1) * each]


def expert_kernel(e, blocks, more, *refs):
    gu, dn, refs = refs[0], refs[1], refs[2:]
    copies = []
    if more:
        copies = fetches(e + 1, *refs[:2], *refs[-5:-3], refs[-1])
        refs = refs[4:-1]
    for c in copies:
        c.start()
    x_refs, y_refs = refs[:blocks], refs[blocks : 2 * blocks]
    x, hidden = refs[-2:]
    hid, width = dn.shape
    rows = x_refs[0].shape[0]
    for b in range(blocks):
        x[b * rows : (b + 1) * rows] = x_refs[b][...]
    for at, size in chunks_of(hid, 256):
        gate, up = [
            lax.dot_general(
                x[...], gu[g, at : at + size], NT, preferred_element_type=jnp.float32
            )
            for g in range(2)
        ]
        act = (up + 1.0) * gate * jax.nn.sigmoid(1.702 * gate)
        hidden[:, at : at + size] = act.astype(jnp.bfloat16)
    for at, size in chunks_of(width, 768):
        part = jnp.dot(
            hidden[...], dn[:, at : at + size], preferred_element_type=jnp.float32
        ).astype(jnp.bfloat16)
        for b in range(blocks):
            y_refs[b][:, at : at + size] = part[b * rows : (b + 1) * rows]
    for c in copies:
        c.wait()


def combine_kernel(exp_dev, chips, pair, cols, high_ref, low_ref, *refs):
    per = chips + (pair - 1)
    ins, refs = refs[: exp_dev * per], refs[exp_dev * per :]
    own_ref, out_refs, flat, mixed = refs[0], refs[1:cols], refs[-2], refs[-1]
    col = lax.axis_index("col")
    at = 0
    for e in range(exp_dev):
        for j in range(chips):
            flat[at : at + CAP] = ins[e * per + j][:CAP]
            at += CAP
        if pair == 2:
            flat[at : at + CAP * chips] = ins[e * per + chips][...]
            at += CAP * chips
    y = flat[...]
    total = lax.dot_general(high_ref[...], y, TN, preferred_element_type=jnp.float32)
    total += lax.dot_general(low_ref[...], y, TN, preferred_element_type=jnp.float32)
    width = own_ref.shape[1]
    for p in range(cols):
        mixed[p] = total[:, p * width : (p + 1) * width]
    own_ref[...] = mixed[col]
    for j in range(1, cols):
        out_refs[j - 1][...] = mixed[dest(col, j, cols)].astype(jnp.bfloat16)


def params(mib):
    return pltpu.CompilerParams(vmem_limit_bytes=mib << 20)


def layer(tokens, route_ids, route_weights, expert_gate_up, expert_down):
    rows, cols = lax.axis_size("row"), lax.axis_size("col")
    pair = 2 if rows % 2 == 0 else 1
    chips = rows // pair
    toks, part_width = tokens.shape
    exp_dev, width, _, hid = expert_gate_up.shape
    slots = exp_dev * rows * CAP
    bf16, f32 = jnp.bfloat16, jnp.float32
    shape = jax.ShapeDtypeStruct

    def over_col(x, j):
        return lax.ppermute(x, "col", [(i, dest(i, j, cols)) for i in range(cols)])

    def over_chips(x, j, back=False):
        to = source if back else dest
        perm = [
            (c * pair + k, to(c, j, chips) * pair + k)
            for c in range(chips)
            for k in range(pair)
        ]
        return lax.ppermute(x, "row", perm)

    def over_cores(x):
        return lax.ppermute(x, "row", [(i, i ^ 1) for i in range(rows)])

    def hold(x):
        return pltpu.with_memory_space_constraint(x, pltpu.HBM)

    far = range(cols - 1, 0, -1)
    others = range(1, chips)
    arrived = {j: over_col(tokens, j) for j in far}
    parts = [tokens] + [arrived[j] for j in range(1, cols)]

    gate_up = hold(jnp.transpose(expert_gate_up, (0, 2, 3, 1)))
    expert_down = hold(expert_down)
    held = [pltpu.VMEM((2, hid, width), bf16), pltpu.VMEM((hid, width), bf16)]
    place, high, low, *weights = pl.pallas_call(
        functools.partial(route_kernel, rows, exp_dev),
        out_shape=[shape((slots, toks), bf16)] * 3 + held * exp_dev,
        in_specs=[HBM] * 4,
        out_specs=[VMEM] * (3 + 2 * exp_dev),
        scratch_shapes=[
            pltpu.VMEM(route_ids.shape[::-1], route_ids.dtype),
            pltpu.VMEM(route_weights.shape[::-1], f32),
            pltpu.SemaphoreType.DMA((4,)),
        ],
        compiler_params=params(4),
        name="route",
    )(hold(route_ids.T), hold(route_weights.T), gate_up, expert_down)

    outs = exp_dev * pair
    sent = pl.pallas_call(
        functools.partial(dispatch_kernel, cols, outs),
        out_shape=[shape((chips * CAP, width), bf16)] * outs,
        in_specs=[VMEM] * (1 + cols),
        out_specs=[VMEM] * outs,
        scratch_shapes=[pltpu.VMEM((toks, width), f32)],
        compiler_params=params(8),
        name="dispatch",
    )(place, *parts)

    block = pair * CAP
    inputs = []
    for e in range(exp_dev):
        halves = [sent[e * pair].reshape(chips, CAP, width)]
        if pair == 2:
            swapped = over_cores(sent[e * pair + 1])
            halves.append(swapped.reshape(chips, CAP, width))
        blocks = [
            jnp.concatenate([h[j] for h in halves], axis=0) for j in range(chips)
        ]
        inputs.append([blocks[0]] + [over_chips(blocks[j], j) for j in others])
    terms = []
    for e in range(exp_dev):
        more = e + 1 < exp_dev
        ys = pl.pallas_call(
            functools.partial(expert_kernel, e, chips, more),
            out_shape=[shape((block, width), bf16)] * chips + held * more,
            in_specs=[VMEM] * 2 + [HBM, HBM, VMEM, VMEM] * more + [VMEM] * chips,
            out_specs=[VMEM] * (chips + 2 * more),
            scratch_shapes=[
                pltpu.VMEM((chips * block, width), bf16),
                pltpu.VMEM((chips * block, hid), bf16),
            ]
            + [pltpu.SemaphoreType.DMA((2,))] * more,
            compiler_params=params(12),
            cost_estimate=pl.CostEstimate(
                flops=6 * chips * block * width * hid,
                bytes_accessed=6 * width * hid,
                transcendentals=chips * block * hid,
            ),
            input_output_aliases={4: chips, 5: chips + 1} if more else {},
        )(*weights[:2], *[gate_up, expert_down, *weights[2:4]] * more, *inputs[e])
        weights = [*ys[chips:], *weights[4:]]
        got = [ys[0]] + [over_chips(ys[j], j, True) for j in others]
        terms += got
        if pair == 2:
            give = jnp.concatenate([g[CAP:] for g in got], axis=0)
            terms.append(over_cores(give))

    own, *leaving = pl.pallas_call(
        functools.partial(combine_kernel, exp_dev, chips, pair, cols),
        out_shape=[shape((toks, part_width), f32)]
        + [shape((toks, part_width), bf16)] * (cols - 1),
        in_specs=[VMEM] * (2 + len(terms)),
        out_specs=[VMEM] * cols,
        scratch_shapes=[
            pltpu.VMEM((slots, width), bf16),
            pltpu.VMEM((cols, toks, part_width), f32),
        ],
        compiler_params=params(16),
        name="combine",
    )(high, low, *terms)
    total = own
    for j in far:
        total = total + over_col(leaving[j - 1], j).astype(f32)
    return total.astype(bf16)


def solution(mesh):
    return jax.shard_map(
        layer,
        mesh=mesh,
        in_specs=(
            P("row", "col"),
            P("row", None),
            P("row", None),
            P("row", None, None, "col"),
            P("row", "col", None),
        ),
        out_specs=P("row", "col"),
        check_vma=False,
    )
```

```python
import functools

import jax
import jax.numpy as jnp
from jax import lax
from jax.experimental import pallas as pl
from jax.experimental.pallas import tpu as pltpu
from jax.sharding import PartitionSpec as P


CAP = 8
NT = (((1,), (1,)), ((), ()))
TN = (((0,), (0,)), ((), ()))
VMEM = pl.BlockSpec(memory_space=pltpu.VMEM)
HBM = pl.BlockSpec(memory_space=pltpu.HBM)


def dest(i, j, n):
    return i ^ j if n & (n - 1) == 0 else (i + j) % n


def source(i, j, n):
    return i ^ j if n & (n - 1) == 0 else (i + n - j) % n


def chunks_of(total, size):
    return [(at, min(size, total - at)) for at in range(0, total, size)]


def fetches(e, gu_hbm, dn_hbm, gu, dn, sems):
    return [
        pltpu.make_async_copy(gu_hbm.at[e], gu, sems.at[0]),
        pltpu.make_async_copy(dn_hbm.at[e], dn, sems.at[1]),
    ]


def route_kernel(rows, exp_dev, ids_hbm, w_hbm, gu_hbm, dn_hbm, *refs):
    place_ref, high_ref, low_ref, gu, dn, *_, ids_ref, w_ref, sems = refs
    small = [
        pltpu.make_async_copy(ids_hbm, ids_ref, sems.at[2]),
        pltpu.make_async_copy(w_hbm, w_ref, sems.at[3]),
    ]
    copies = fetches(0, gu_hbm, dn_hbm, gu, dn, sems)
    for c in small + copies:
        c.start()
    pair = 2 if rows % 2 == 0 else 1
    chips = rows // pair
    me = lax.axis_index("row")
    top, toks = ids_ref.shape
    experts = rows * exp_dev
    at = lax.broadcasted_iota(jnp.int32, (experts, 1), 0)
    e, q, j = at // rows, (at // chips) % pair, at % chips
    chip = dest(jnp.full_like(at, me // pair), j, chips)
    core = jnp.full_like(at, me % pair) ^ q
    expert = (chip * pair + core) * exp_dev + e
    hit = jnp.zeros((experts, toks), jnp.float32)
    weight = jnp.zeros((experts, toks), jnp.float32)
    for c in small:
        c.wait()
    for k in range(top):
        same = (ids_ref[k : k + 1, :] == expert).astype(jnp.float32)
        hit += same
        weight += same * w_ref[k : k + 1, :]
    earlier = lax.broadcasted_iota(jnp.int32, (toks, toks), 0)
    later = lax.broadcasted_iota(jnp.int32, (toks, toks), 1)
    before = jnp.dot(
        hit.astype(jnp.bfloat16),
        (earlier < later).astype(jnp.bfloat16),
        preferred_element_type=jnp.float32,
    )
    slot = jnp.where(hit > 0.0, before, -1.0)
    spread = lambda a: jnp.broadcast_to(a[:, None, :], (experts, CAP, toks)).reshape(
        experts * CAP, toks
    )
    want = lax.broadcasted_iota(jnp.int32, (experts * CAP, toks), 0) % CAP
    place = (spread(slot) == want.astype(jnp.float32)).astype(jnp.float32)
    value = place * spread(weight)
    high = value.astype(jnp.bfloat16)
    place_ref[...] = place.astype(jnp.bfloat16)
    high_ref[...] = high
    low_ref[...] = (value - high.astype(jnp.float32)).astype(jnp.bfloat16)
    for c in copies:
        c.wait()


def dispatch_kernel(cols, outs, place_ref, *refs):
    part_refs, out_refs, whole = refs[:cols], refs[cols : cols + outs], refs[-1]
    col = lax.axis_index("col")
    width = part_refs[0].shape[1]
    parts = [r[...] for r in part_refs]
    for p in range(cols):
        j = source(col, p, cols) if cols & (cols - 1) == 0 else (col + cols - p) % cols
        part = parts[0]
        for other in range(1, cols):
            part = jnp.where(j == other, parts[other], part)
        whole[:, p * width : (p + 1) * width] = part.astype(jnp.float32)
    full = whole[...].astype(jnp.bfloat16)
    sent = jnp.dot(place_ref[...], full, preferred_element_type=jnp.float32)
    sent = sent.astype(jnp.bfloat16)
    each = sent.shape[0] // outs
    for i in range(outs):
        out_refs[i][...] = sent[i * each : (i + 1) * each]


def expert_kernel(e, blocks, more, *refs):
    gu, dn, refs = refs[0], refs[1], refs[2:]
    copies = []
    if more:
        copies = fetches(e + 1, *refs[:2], *refs[-5:-3], refs[-1])
        refs = refs[4:-1]
    for c in copies:
        c.start()
    x_refs, y_refs = refs[:blocks], refs[blocks : 2 * blocks]
    x, hidden = refs[-2:]
    hid, width = dn.shape
    rows = x_refs[0].shape[0]
    for b in range(blocks):
        x[b * rows : (b + 1) * rows] = x_refs[b][...]
    for at, size in chunks_of(hid, 256):
        gate, up = [
            lax.dot_general(
                x[...], gu[g, at : at + size], NT, preferred_element_type=jnp.float32
            )
            for g in range(2)
        ]
        act = (up + 1.0) * gate * jax.nn.sigmoid(1.702 * gate)
        hidden[:, at : at + size] = act.astype(jnp.bfloat16)
    for at, size in chunks_of(width, 768):
        part = jnp.dot(
            hidden[...], dn[:, at : at + size], preferred_element_type=jnp.float32
        ).astype(jnp.bfloat16)
        for b in range(blocks):
            y_refs[b][:, at : at + size] = part[b * rows : (b + 1) * rows]
    for c in copies:
        c.wait()


def combine_kernel(exp_dev, chips, pair, cols, high_ref, low_ref, *refs):
    ins, refs = refs[: chips + pair - 1], refs[chips + pair - 1 :]
    own_ref, out_refs, flat, mixed = refs[0], refs[1:cols], refs[-2], refs[-1]
    col = lax.axis_index("col")
    for e in range(exp_dev):
        for q in range(pair):
            for j in range(chips):
                piece = ins[chips] if q else ins[j]
                at = ((q * j) * exp_dev + e) * CAP
                to = ((e * pair + q) * chips + j) * CAP
                flat[to : to + CAP] = piece[at : at + CAP]
    y = flat[...]
    total = lax.dot_general(high_ref[...], y, TN, preferred_element_type=jnp.float32)
    total += lax.dot_general(low_ref[...], y, TN, preferred_element_type=jnp.float32)
    width = own_ref.shape[1]
    for p in range(cols):
        mixed[p] = total[:, p * width : (p + 1) * width]
    own_ref[...] = mixed[col]
    for j in range(1, cols):
        out_refs[j - 1][...] = mixed[dest(col, j, cols)].astype(jnp.bfloat16)


def params(mib):
    return pltpu.CompilerParams(vmem_limit_bytes=mib << 20)


def layer(tokens, route_ids, route_weights, expert_gate_up, expert_down):
    rows, cols = lax.axis_size("row"), lax.axis_size("col")
    pair = 2 if rows % 2 == 0 else 1
    chips = rows // pair
    toks, part_width = tokens.shape
    exp_dev, width, _, hid = expert_gate_up.shape
    slots = exp_dev * rows * CAP
    bf16, f32 = jnp.bfloat16, jnp.float32
    shape = jax.ShapeDtypeStruct

    def over_col(x, j):
        return lax.ppermute(x, "col", [(i, dest(i, j, cols)) for i in range(cols)])

    def over_chips(x, j, back=False):
        to = source if back else dest
        perm = [
            (c * pair + k, to(c, j, chips) * pair + k)
            for c in range(chips)
            for k in range(pair)
        ]
        return lax.ppermute(x, "row", perm)

    def over_cores(x):
        return lax.ppermute(x, "row", [(i, i ^ 1) for i in range(rows)])

    def hold(x):
        return pltpu.with_memory_space_constraint(x, pltpu.HBM)

    far = range(cols - 1, 0, -1)
    others = range(1, chips)
    arrived = {j: over_col(tokens, j) for j in far}
    parts = [tokens] + [arrived[j] for j in range(1, cols)]

    gate_up = hold(jnp.transpose(expert_gate_up, (0, 2, 3, 1)))
    expert_down = hold(expert_down)
    held = [pltpu.VMEM((2, hid, width), bf16), pltpu.VMEM((hid, width), bf16)]
    place, high, low, *weights = pl.pallas_call(
        functools.partial(route_kernel, rows, exp_dev),
        out_shape=[shape((slots, toks), bf16)] * 3 + held * exp_dev,
        in_specs=[HBM] * 4,
        out_specs=[VMEM] * (3 + 2 * exp_dev),
        scratch_shapes=[
            pltpu.VMEM(route_ids.shape[::-1], route_ids.dtype),
            pltpu.VMEM(route_weights.shape[::-1], f32),
            pltpu.SemaphoreType.DMA((4,)),
        ],
        compiler_params=params(4),
        name="route",
    )(hold(route_ids.T), hold(route_weights.T), gate_up, expert_down)

    outs = exp_dev * pair
    sent = pl.pallas_call(
        functools.partial(dispatch_kernel, cols, outs),
        out_shape=[shape((chips * CAP, width), bf16)] * outs,
        in_specs=[VMEM] * (1 + cols),
        out_specs=[VMEM] * outs,
        scratch_shapes=[pltpu.VMEM((toks, width), f32)],
        compiler_params=params(8),
        name="dispatch",
    )(place, *parts)

    block = pair * CAP
    inputs = []
    for e in range(exp_dev):
        halves = [sent[e * pair].reshape(chips, CAP, width)]
        if pair == 2:
            swapped = over_cores(sent[e * pair + 1])
            halves.append(swapped.reshape(chips, CAP, width))
        blocks = [
            jnp.concatenate([h[j] for h in halves], axis=0) for j in range(chips)
        ]
        inputs.append([blocks[0]] + [over_chips(blocks[j], j) for j in others])
    made = []
    for e in range(exp_dev):
        more = e + 1 < exp_dev
        ys = pl.pallas_call(
            functools.partial(expert_kernel, e, chips, more),
            out_shape=[shape((block, width), bf16)] * chips + held * more,
            in_specs=[VMEM] * 2 + [HBM, HBM, VMEM, VMEM] * more + [VMEM] * chips,
            out_specs=[VMEM] * (chips + 2 * more),
            scratch_shapes=[
                pltpu.VMEM((chips * block, width), bf16),
                pltpu.VMEM((chips * block, hid), bf16),
            ]
            + [pltpu.SemaphoreType.DMA((2,))] * more,
            compiler_params=params(12),
            cost_estimate=pl.CostEstimate(
                flops=6 * chips * block * width * hid,
                bytes_accessed=6 * width * hid,
                transcendentals=chips * block * hid,
            ),
            input_output_aliases={4: chips, 5: chips + 1} if more else {},
        )(*weights[:2], *[gate_up, expert_down, *weights[2:4]] * more, *inputs[e])
        weights = [*ys[chips:], *weights[4:]]
        made.append(ys[:chips])

    def of_core(j, q):
        rows = [made[e][j][q * CAP : (q + 1) * CAP] for e in range(exp_dev)]
        return jnp.concatenate(rows, axis=0)

    terms = []
    if pair == 2:
        passed = [of_core(0, 1)] + [over_chips(of_core(j, 1), j, True) for j in others]
        terms = [over_cores(jnp.concatenate(passed, axis=0))]
    near = [of_core(0, 0)] + [over_chips(of_core(j, 0), j, True) for j in others]
    terms = [*near, *terms]

    own, *leaving = pl.pallas_call(
        functools.partial(combine_kernel, exp_dev, chips, pair, cols),
        out_shape=[shape((toks, part_width), f32)]
        + [shape((toks, part_width), bf16)] * (cols - 1),
        in_specs=[VMEM] * (2 + len(terms)),
        out_specs=[VMEM] * cols,
        scratch_shapes=[
            pltpu.VMEM((slots, width), bf16),
            pltpu.VMEM((cols, toks, part_width), f32),
        ],
        compiler_params=params(16),
        name="combine",
    )(high, low, *terms)
    total = own
    for j in far:
        total = total + over_col(leaving[j - 1], j).astype(f32)
    return total.astype(bf16)


def solution(mesh):
    return jax.shard_map(
        layer,
        mesh=mesh,
        in_specs=(
            P("row", "col"),
            P("row", None),
            P("row", None),
            P("row", None, None, "col"),
            P("row", "col", None),
        ),
        out_specs=P("row", "col"),
        check_vma=False,
    )
```

```python
import functools

import jax
import jax.numpy as jnp
from jax import lax
from jax.experimental import pallas as pl
from jax.experimental.pallas import tpu as pltpu
from jax.sharding import PartitionSpec as P


CAP = 8
NT = (((1,), (1,)), ((), ()))
TN = (((0,), (0,)), ((), ()))
VMEM = pl.BlockSpec(memory_space=pltpu.VMEM)
HBM = pl.BlockSpec(memory_space=pltpu.HBM)


def dest(i, j, n):
    return i ^ j if n & (n - 1) == 0 else (i + j) % n


def source(i, j, n):
    return i ^ j if n & (n - 1) == 0 else (i + n - j) % n


def chunks_of(total, size):
    return [(at, min(size, total - at)) for at in range(0, total, size)]


def fetches(e, gu_hbm, dn_hbm, gu, dn, sems):
    return [
        pltpu.make_async_copy(gu_hbm.at[e], gu, sems.at[0]),
        pltpu.make_async_copy(dn_hbm.at[e], dn, sems.at[1]),
    ]


def route_kernel(rows, exp_dev, ids_hbm, w_hbm, gu_hbm, dn_hbm, *refs):
    place_ref, high_ref, low_ref, gu, dn, *_, ids_ref, w_ref, sems = refs
    small = [
        pltpu.make_async_copy(ids_hbm, ids_ref, sems.at[2]),
        pltpu.make_async_copy(w_hbm, w_ref, sems.at[3]),
    ]
    copies = fetches(0, gu_hbm, dn_hbm, gu, dn, sems)
    for c in small + copies:
        c.start()
    pair = 2 if rows % 2 == 0 else 1
    chips = rows // pair
    me = lax.axis_index("row")
    top, toks = ids_ref.shape
    experts = rows * exp_dev
    at = lax.broadcasted_iota(jnp.int32, (experts, 1), 0)
    e, q, j = at // rows, (at // chips) % pair, at % chips
    chip = dest(jnp.full_like(at, me // pair), j, chips)
    core = jnp.full_like(at, me % pair) ^ q
    expert = (chip * pair + core) * exp_dev + e
    hit = jnp.zeros((experts, toks), jnp.float32)
    weight = jnp.zeros((experts, toks), jnp.float32)
    for c in small:
        c.wait()
    for k in range(top):
        same = (ids_ref[k : k + 1, :] == expert).astype(jnp.float32)
        hit += same
        weight += same * w_ref[k : k + 1, :]
    earlier = lax.broadcasted_iota(jnp.int32, (toks, toks), 0)
    later = lax.broadcasted_iota(jnp.int32, (toks, toks), 1)
    before = jnp.dot(
        hit.astype(jnp.bfloat16),
        (earlier < later).astype(jnp.bfloat16),
        preferred_element_type=jnp.float32,
    )
    slot = jnp.where(hit > 0.0, before, -1.0)
    spread = lambda a: jnp.broadcast_to(a[:, None, :], (experts, CAP, toks)).reshape(
        experts * CAP, toks
    )
    want = lax.broadcasted_iota(jnp.int32, (experts * CAP, toks), 0) % CAP
    place = (spread(slot) == want.astype(jnp.float32)).astype(jnp.float32)
    value = place * spread(weight)
    high = value.astype(jnp.bfloat16)
    place_ref[...] = place.astype(jnp.bfloat16)
    high_ref[...] = high
    low_ref[...] = (value - high.astype(jnp.float32)).astype(jnp.bfloat16)
    for c in copies:
        c.wait()


def dispatch_kernel(cols, outs, place_ref, *refs):
    part_refs, out_refs, whole = refs[:cols], refs[cols : cols + outs], refs[-1]
    col = lax.axis_index("col")
    width = part_refs[0].shape[1]
    parts = [r[...] for r in part_refs]
    for p in range(cols):
        j = source(col, p, cols) if cols & (cols - 1) == 0 else (col + cols - p) % cols
        part = parts[0]
        for other in range(1, cols):
            part = jnp.where(j == other, parts[other], part)
        whole[:, p * width : (p + 1) * width] = part.astype(jnp.float32)
    full = whole[...].astype(jnp.bfloat16)
    sent = jnp.dot(place_ref[...], full, preferred_element_type=jnp.float32)
    sent = sent.astype(jnp.bfloat16)
    each = sent.shape[0] // outs
    for i in range(outs):
        out_refs[i][...] = sent[i * each : (i + 1) * each]


def expert_kernel(e, blocks, more, gu_hbm, dn_hbm, gu, dn, *refs):
    refs = refs[more:]
    x_refs, y_refs, refs = refs[:blocks], refs[blocks : 2 * blocks], refs[2 * blocks :]
    x, hidden, sems = refs[-3:]
    down, ahead = [], []
    if e > 0:
        dn = refs[0]
        down = [pltpu.make_async_copy(dn_hbm.at[e], dn, sems.at[0])]
    if more:
        next_gu = refs[-4]
        ahead = [pltpu.make_async_copy(gu_hbm.at[e + 1], next_gu, sems.at[1])]
    for c in down + ahead:
        c.start()
    hid, width = dn.shape
    rows = x_refs[0].shape[0]
    for b in range(blocks):
        x[b * rows : (b + 1) * rows] = x_refs[b][...]
    for at, size in chunks_of(hid, 256):
        gate, up = [
            lax.dot_general(
                x[...], gu[g, at : at + size], NT, preferred_element_type=jnp.float32
            )
            for g in range(2)
        ]
        act = (up + 1.0) * gate * jax.nn.sigmoid(1.702 * gate)
        hidden[:, at : at + size] = act.astype(jnp.bfloat16)
    for c in down:
        c.wait()
    for at, size in chunks_of(width, 768):
        part = jnp.dot(
            hidden[...], dn[:, at : at + size], preferred_element_type=jnp.float32
        ).astype(jnp.bfloat16)
        for b in range(blocks):
            y_refs[b][:, at : at + size] = part[b * rows : (b + 1) * rows]
    for c in ahead:
        c.wait()


def combine_kernel(exp_dev, chips, pair, cols, high_ref, low_ref, *refs):
    ins, refs = refs[: chips + pair - 1], refs[chips + pair - 1 :]
    own_ref, out_refs, flat, mixed = refs[0], refs[1:cols], refs[-2], refs[-1]
    col = lax.axis_index("col")
    for e in range(exp_dev):
        for q in range(pair):
            for j in range(chips):
                piece = ins[chips] if q else ins[j]
                at = ((q * j) * exp_dev + e) * CAP
                to = ((e * pair + q) * chips + j) * CAP
                flat[to : to + CAP] = piece[at : at + CAP]
    y = flat[...]
    total = lax.dot_general(high_ref[...], y, TN, preferred_element_type=jnp.float32)
    total += lax.dot_general(low_ref[...], y, TN, preferred_element_type=jnp.float32)
    width = own_ref.shape[1]
    for p in range(cols):
        mixed[p] = total[:, p * width : (p + 1) * width]
    own_ref[...] = mixed[col]
    for j in range(1, cols):
        out_refs[j - 1][...] = mixed[dest(col, j, cols)].astype(jnp.bfloat16)


def params(mib):
    return pltpu.CompilerParams(vmem_limit_bytes=mib << 20)


def layer(tokens, route_ids, route_weights, expert_gate_up, expert_down):
    rows, cols = lax.axis_size("row"), lax.axis_size("col")
    pair = 2 if rows % 2 == 0 else 1
    chips = rows // pair
    toks, part_width = tokens.shape
    exp_dev, width, _, hid = expert_gate_up.shape
    slots = exp_dev * rows * CAP
    bf16, f32 = jnp.bfloat16, jnp.float32
    shape = jax.ShapeDtypeStruct

    def over_col(x, j):
        return lax.ppermute(x, "col", [(i, dest(i, j, cols)) for i in range(cols)])

    def over_chips(x, j, back=False):
        to = source if back else dest
        perm = [
            (c * pair + k, to(c, j, chips) * pair + k)
            for c in range(chips)
            for k in range(pair)
        ]
        return lax.ppermute(x, "row", perm)

    def over_cores(x):
        return lax.ppermute(x, "row", [(i, i ^ 1) for i in range(rows)])

    def hold(x):
        return pltpu.with_memory_space_constraint(x, pltpu.HBM)

    far = range(cols - 1, 0, -1)
    others = range(1, chips)
    arrived = {j: over_col(tokens, j) for j in far}
    parts = [tokens] + [arrived[j] for j in range(1, cols)]

    gate_up = hold(jnp.transpose(expert_gate_up, (0, 2, 3, 1)))
    expert_down = hold(expert_down)
    held = [pltpu.VMEM((2, hid, width), bf16), pltpu.VMEM((hid, width), bf16)]
    place, high, low, *weights = pl.pallas_call(
        functools.partial(route_kernel, rows, exp_dev),
        out_shape=[shape((slots, toks), bf16)] * 3 + held * exp_dev,
        in_specs=[HBM] * 4,
        out_specs=[VMEM] * (3 + 2 * exp_dev),
        scratch_shapes=[
            pltpu.VMEM(route_ids.shape[::-1], route_ids.dtype),
            pltpu.VMEM(route_weights.shape[::-1], f32),
            pltpu.SemaphoreType.DMA((4,)),
        ],
        compiler_params=params(4),
        name="route",
    )(hold(route_ids.T), hold(route_weights.T), gate_up, expert_down)

    outs = exp_dev * pair
    sent = pl.pallas_call(
        functools.partial(dispatch_kernel, cols, outs),
        out_shape=[shape((chips * CAP, width), bf16)] * outs,
        in_specs=[VMEM] * (1 + cols),
        out_specs=[VMEM] * outs,
        scratch_shapes=[pltpu.VMEM((toks, width), f32)],
        compiler_params=params(8),
        name="dispatch",
    )(place, *parts)

    block = pair * CAP
    inputs = []
    for e in range(exp_dev):
        halves = [sent[e * pair].reshape(chips, CAP, width)]
        if pair == 2:
            swapped = over_cores(sent[e * pair + 1])
            halves.append(swapped.reshape(chips, CAP, width))
        blocks = [
            jnp.concatenate([h[j] for h in halves], axis=0) for j in range(chips)
        ]
        inputs.append([blocks[0]] + [over_chips(blocks[j], j) for j in others])
    made = []
    for e in range(exp_dev):
        more = e + 1 < exp_dev
        gu, dn = weights[2 * e : 2 * e + 2]
        filled = [held[1]] * (e > 0) + [held[0]] * more
        ys = pl.pallas_call(
            functools.partial(expert_kernel, e, chips, more),
            out_shape=[shape((block, width), bf16)] * chips + filled,
            in_specs=[HBM] * 2 + [VMEM] * (2 + more + chips),
            out_specs=[VMEM] * (chips + len(filled)),
            scratch_shapes=[
                pltpu.VMEM((chips * block, width), bf16),
                pltpu.VMEM((chips * block, hid), bf16),
                pltpu.SemaphoreType.DMA((2,)),
            ],
            compiler_params=params(12),
            cost_estimate=pl.CostEstimate(
                flops=6 * chips * block * width * hid,
                bytes_accessed=6 * width * hid,
                transcendentals=chips * block * hid,
            ),
            input_output_aliases=({3: chips} if e > 0 else {})
            | ({4: chips + (e > 0)} if more else {}),
        )(gate_up, expert_down, gu, dn, *weights[2 * e + 2 : 2 * e + 2 + more], *inputs[e])
        if more:
            weights = [*weights[: 2 * e + 2], ys[-1], *weights[2 * e + 3 :]]
        made.append(ys[:chips])

    def of_core(j, q):
        rows = [made[e][j][q * CAP : (q + 1) * CAP] for e in range(exp_dev)]
        return jnp.concatenate(rows, axis=0)

    terms = []
    if pair == 2:
        passed = [of_core(0, 1)] + [over_chips(of_core(j, 1), j, True) for j in others]
        terms = [over_cores(jnp.concatenate(passed, axis=0))]
    near = [of_core(0, 0)] + [over_chips(of_core(j, 0), j, True) for j in others]
    terms = [*near, *terms]

    own, *leaving = pl.pallas_call(
        functools.partial(combine_kernel, exp_dev, chips, pair, cols),
        out_shape=[shape((toks, part_width), f32)]
        + [shape((toks, part_width), bf16)] * (cols - 1),
        in_specs=[VMEM] * (2 + len(terms)),
        out_specs=[VMEM] * cols,
        scratch_shapes=[
            pltpu.VMEM((slots, width), bf16),
            pltpu.VMEM((cols, toks, part_width), f32),
        ],
        compiler_params=params(16),
        name="combine",
    )(high, low, *terms)
    total = own
    for j in far:
        total = total + over_col(leaving[j - 1], j).astype(f32)
    return total.astype(bf16)


def solution(mesh):
    return jax.shard_map(
        layer,
        mesh=mesh,
        in_specs=(
            P("row", "col"),
            P("row", None),
            P("row", None),
            P("row", None, None, "col"),
            P("row", "col", None),
        ),
        out_specs=P("row", "col"),
        check_vma=False,
    )
```
